32 devices in a mesh: layer: 2 (over core), tok: 16 (over z, y, x).
Axes of the slice: x: 2, y: 2, z: 4, core: 2. Of those that a mesh axis runs over, the one named last changes fastest.
Arguments:
- train_act: bfloat16 [4, 32768, 256], P('layer', 'tok'), may hold values from -0.75 to 0.75
- train_grad: bfloat16 [4, 32768, 256], P('layer', 'tok'), may hold values from -0.75 to 0.75
- test_act: bfloat16 [4, 2048, 256], P('layer', 'tok'), may hold values from -0.75 to 0.75
- test_grad: bfloat16 [4, 2048, 256], P('layer', 'tok'), may hold values from -0.75 to 0.75
- segment_ids: int32 [2048], replicated, may hold values from 0 to 127, as said below
Outputs:
- scores: float32 [128, 32768], P('layer', 'tok')
The draws below stay inside these ranges and needn't reach their ends.
Inputs may be any that keep to these rules, and one draw needn't show every extreme that they name: `segment_ids`: each of the 128 queries has exactly 16 test tokens, placed anywhere among the 2048.
All inputs are finite; a program needn't handle non-finite values.
Results may differ from the reference program's by a relative error of at most 0.0029.
Values may be sent and summed in bfloat16 or wider, within the bound.
A program may use at most 128 MiB of HBM per device.

```python
import jax
import jax.numpy as jnp
from jax import lax

P_SIZE = 256
Q = 128
QTOK = 16
S = 2048
L = 4
TOKENS = 32768


def draw_segment_ids(key, part):
    order = jax.random.permutation(jax.random.fold_in(key, 7), S)
    return (order // QTOK).astype(jnp.int32)


def steps_of(own_key, dims, cuts, low, top_value):
    def one(position, blocks):
        heights = jax.random.uniform(jax.random.fold_in(jax.random.fold_in(own_key, 6), position), (blocks,), jnp.float32, low / len(cuts), top_value / len(cuts))
        return jnp.repeat(jnp.exp(heights), dims[position] // blocks).reshape((-1,) + (1,) * (len(dims) - position - 1))

    level = one(*cuts[0])
    for cut in cuts[1:]:
        level = level * one(*cut)
    return level


def bell_draw(key, shape, deviation, reach, pieces=(), kind=jnp.bfloat16):
    values = jax.random.normal(key, shape, jnp.float32) * deviation
    if len(pieces) > 0:
        values = steps_of(key, shape, pieces, -0.22, 0.18) * values
    return jnp.clip(values, min=-reach, max=reach).astype(kind)


def setup_inputs(seed: int = 0) -> dict:
    keys = jax.random.split(jax.random.key(seed), 6)
    return {
        "train_act": bell_draw(keys[0], (L, TOKENS, P_SIZE), 0.125, 0.75, ((0, 2), (1, 16))),
        "train_grad": bell_draw(keys[1], (L, TOKENS, P_SIZE), 0.125, 0.75, ((0, 2), (1, 16))),
        "test_act": bell_draw(keys[2], (L, S, P_SIZE), 0.125, 0.75, ((0, 2), (1, 16))),
        "test_grad": bell_draw(keys[3], (L, S, P_SIZE), 0.125, 0.75, ((0, 2), (1, 16))),
        "segment_ids": draw_segment_ids(jax.random.fold_in(keys[5], 71), 0),
    }


def reference(train_act, train_grad, test_act, test_grad, segment_ids):
    labels = jnp.arange(Q, dtype=jnp.int32)[:, None]
    select = (segment_ids[None, :] == labels).astype(jnp.bfloat16)

    def one_layer(running, tensors):
        act_train, grad_train, act_test, grad_test = tensors
        act_gram = jnp.einsum("sp,tp->st", act_test.astype(jnp.float32), act_train.astype(jnp.float32))
        grad_gram = jnp.einsum("sp,tp->st", grad_test.astype(jnp.float32), grad_train.astype(jnp.float32))
        product = (act_gram * grad_gram).astype(jnp.bfloat16)
        return running + jnp.dot(select, product, preferred_element_type=jnp.float32), None

    initial = jnp.zeros((Q, train_act.shape[1]), jnp.float32)
    scores, _ = lax.scan(one_layer, initial, (train_act, train_grad, test_act, test_grad))
    return scores
```

```python
import functools
import math

import jax
import jax.numpy as jnp
from jax import lax
from jax.experimental import pallas as pl
from jax.experimental.pallas import tpu as pltpu
from jax.sharding import PartitionSpec as P

Q = 128
MESH = pl.DeviceIdType.MESH


def kernel(
    layers,
    line,
    train_a,
    train_g,
    test_a,
    test_g,
    ids_ref,
    out_ref,
    ta,
    tg,
    buf,
    acc,
    xbuf,
    train_sem,
    own_sem,
    recv_sem,
    send_sem,
    xs_sem,
    xr_sem,
):
    me = lax.axis_index("tok")
    core = lax.axis_index("layer")
    z = me // 4
    y = (me // 2) % 2
    x = me % 2
    own_col = y * 2 + x
    x_col = y * 2 + (1 - x)
    y_col = (1 - y) * 2 + x
    d_col = (1 - y) * 2 + (1 - x)
    x_dev = z * 4 + x_col
    y_dev = z * 4 + y_col
    has_up = z < line - 1
    has_down = z > 0
    layer_count, train_rows, _ = ta.shape
    rows = buf.shape[3]
    q_block = Q // layers

    for which, (src, dst) in enumerate(((train_a, ta), (train_g, tg))):
        pltpu.make_async_copy(src, dst, train_sem.at[which]).start()
    for which, src in enumerate((test_a, test_g)):
        pltpu.make_async_copy(src, buf.at[which, me], own_sem.at[which]).start()

    barrier = pltpu.get_barrier_semaphore()

    def greet(where):
        pl.semaphore_signal(barrier, inc=1, device_id=where, device_id_type=MESH)

    greet({"tok": x_dev})
    greet({"tok": y_dev})
    pl.when(has_up)(lambda: greet({"tok": me + 4}))
    pl.when(has_down)(lambda: greet({"tok": me - 4}))
    for step in range(1, layers):
        greet({"layer": lax.rem(core + step, layers)})
    ends = jnp.where(has_up, 1, 0) + jnp.where(has_down, 1, 0)
    pl.semaphore_wait(barrier, layers + 1 + ends)

    def copy(route, which, zz, peer, to, src=None):
        return pltpu.make_async_remote_copy(
            src_ref=buf.at[which, peer] if src is None else src,
            dst_ref=buf.at[which, peer],
            send_sem=send_sem.at[route, which, zz],
            recv_sem=recv_sem.at[which, peer],
            device_id={"tok": to},
            device_id_type=MESH,
        )

    def arrived(which, peer):
        copy(0, which, 0, peer, x_dev).wait_recv()

    def nth(i):
        low = z < line - 1 - z
        near = jnp.where(low, z, line - 1 - z)
        half = (i + 1) // 2
        side = jnp.where(i % 2 == 1, z - half, z + half)
        rest = jnp.where(low, i, line - 1 - i)
        return jnp.where(i <= 2 * near, side, rest)

    for which, src in enumerate((test_a, test_g)):
        pl.when(has_up)(lambda: copy(3, which, z, me, me + 4, src).start())
        pl.when(has_down)(lambda: copy(4, which, z, me, me - 4, src).start())
        copy(0, which, z, me, x_dev, src).start()
        copy(1, which, z, me, y_dev, src).start()

    acc[...] = jnp.zeros_like(acc)
    tile = math.gcd(train_rows, 512)
    labels = lax.broadcasted_iota(jnp.int32, (Q, rows), 0)
    nt = (((1,), (1,)), ((), ()))

    def accumulate(peer):
        select = jnp.where(ids_ref[peer] == labels, 1.0, 0.0).astype(jnp.bfloat16)

        def one_tile(j, carry):
            at = pl.ds(pl.multiple_of(j * tile, tile), tile)
            product = None
            for layer in range(layer_count):
                a_gram = lax.dot_general(
                    buf[0, peer, layer], ta[layer, at, :], nt, preferred_element_type=jnp.float32
                )
                g_gram = lax.dot_general(
                    buf[1, peer, layer], tg[layer, at, :], nt, preferred_element_type=jnp.float32
                )
                term = a_gram * g_gram
                product = term if product is None else product + term
            acc[:, at] += jnp.dot(
                select, product.astype(jnp.bfloat16), preferred_element_type=jnp.float32
            )
            return carry

        lax.fori_loop(0, train_rows // tile, one_tile, 0)

    for which, (src, dst) in enumerate(((train_a, ta), (train_g, tg))):
        pltpu.make_async_copy(src, dst, train_sem.at[which]).wait()
    for which, src in enumerate((test_a, test_g)):
        pltpu.make_async_copy(src, buf.at[which, me], own_sem.at[which]).wait()

    def stage(i, carry):
        zi = nth(i)

        @pl.when(i < line)
        def _():
            accumulate(zi * 4 + own_col)

        @pl.when(i + 1 < line)
        def _():
            zn = nth(i + 1)
            peer = zn * 4 + own_col
            for which in range(2):
                arrived(which, peer)
                pl.when((zn < z) & has_up)(lambda: copy(3, which, zn, peer, me + 4).start())
                pl.when((zn > z) & has_down)(lambda: copy(4, which, zn, peer, me - 4).start())
                copy(0, which, zn, peer, x_dev).start()
                copy(1, which, zn, peer, y_dev).start()

        @pl.when(i < line)
        def _():
            from_x = zi * 4 + x_col
            from_y = zi * 4 + y_col
            arrived(0, from_x)
            copy(2, 0, zi, from_x, y_dev).start()
            arrived(0, from_y)
            arrived(1, from_y)
            copy(2, 1, zi, from_y, x_dev).start()
            arrived(1, from_x)

            def both(k, c):
                accumulate(jnp.where(k == 0, from_x, from_y))
                return c

            lax.fori_loop(0, 2, both, 0)

        @pl.when(i > 0)
        def _():
            peer = nth(i - 1) * 4 + d_col
            arrived(0, peer)
            arrived(1, peer)
            accumulate(peer)

        return carry

    lax.fori_loop(0, line + 1, stage, 0)

    def exchange(step):
        to = lax.rem(core + step, layers)
        return pltpu.make_async_remote_copy(
            src_ref=acc.at[pl.ds(pl.multiple_of(to * q_block, q_block), q_block)],
            dst_ref=xbuf.at[step - 1],
            send_sem=xs_sem.at[step - 1],
            recv_sem=xr_sem.at[step - 1],
            device_id={"layer": to},
            device_id_type=MESH,
        )

    for step in range(1, layers):
        exchange(step).start()

    def drain(zz, carry):
        for which in range(2):
            peer = zz * 4 + own_col
            copy(0, which, zz, peer, x_dev).wait_send()
            copy(1, which, zz, peer, y_dev).wait_send()
            copy(2, which, zz, peer, y_dev).wait_send()
            pl.when((zz <= z) & has_up)(lambda: copy(3, which, zz, peer, me + 4).wait_send())
            pl.when((zz >= z) & has_down)(lambda: copy(4, which, zz, peer, me - 4).wait_send())
        return carry

    lax.fori_loop(0, line, drain, 0)

    mine = pl.ds(pl.multiple_of(core * q_block, q_block), q_block)
    for step in range(1, layers):
        exchange(step).wait_recv()
    result = acc[mine, :]
    for step in range(1, layers):
        result = result + xbuf[step - 1]
    out_ref[...] = result
    for step in range(1, layers):
        exchange(step).wait_send()


def on_device(layers, toks, train_act, train_grad, test_act, test_grad, segment_ids):
    layer_count, train_rows, width = train_act.shape
    rows = test_act.shape[1]
    line = toks // 4
    q_block = Q // layers
    ids = segment_ids.reshape(toks, 1, rows)
    dma = pltpu.SemaphoreType.DMA
    anywhere = pl.BlockSpec(memory_space=pl.ANY)
    return pl.pallas_call(
        functools.partial(kernel, layers, line),
        out_shape=jax.ShapeDtypeStruct((q_block, train_rows), jnp.float32),
        in_specs=[anywhere] * 4 + [pl.BlockSpec(memory_space=pltpu.VMEM)],
        out_specs=pl.BlockSpec(memory_space=pltpu.VMEM),
        scratch_shapes=[
            pltpu.VMEM((layer_count, train_rows, width), jnp.bfloat16),
            pltpu.VMEM((layer_count, train_rows, width), jnp.bfloat16),
            pltpu.VMEM((2, toks, layer_count, rows, width), jnp.bfloat16),
            pltpu.VMEM((Q, train_rows), jnp.float32),
            pltpu.VMEM((layers - 1, q_block, train_rows), jnp.float32),
            dma((2,)),
            dma((2,)),
            dma((2, toks)),
            dma((5, 2, line)),
            dma((layers - 1,)),
            dma((layers - 1,)),
        ],
        compiler_params=pltpu.CompilerParams(
            collective_id=0, has_side_effects=True, vmem_limit_bytes=63 * 1024 * 1024
        ),
    )(train_act, train_grad, test_act, test_grad, ids)


def solution(mesh):
    placed = (
        P("layer", "tok", None),
        P("layer", "tok", None),
        P("layer", "tok", None),
        P("layer", "tok", None),
        P(),
    )
    body = functools.partial(on_device, mesh.shape["layer"], mesh.shape["tok"])
    return jax.shard_map(
        body, mesh=mesh, in_specs=placed, out_specs=P("layer", "tok"), check_vma=False
    )
```

```python
import functools
import math

import jax
import jax.numpy as jnp
from jax import lax
from jax.experimental import pallas as pl
from jax.experimental.pallas import tpu as pltpu
from jax.sharding import PartitionSpec as P

Q = 128
MESH = pl.DeviceIdType.MESH


def kernel(
    layers,
    line,
    train_a,
    train_g,
    test_a,
    test_g,
    ids_ref,
    out_ref,
    ta,
    tg,
    buf,
    acc,
    xbuf,
    train_sem,
    own_sem,
    recv_sem,
    send_sem,
    xs_sem,
    xr_sem,
):
    me = lax.axis_index("tok")
    core = lax.axis_index("layer")
    z = me // 4
    y = (me // 2) % 2
    x = me % 2
    own_col = y * 2 + x
    x_col = y * 2 + (1 - x)
    y_col = (1 - y) * 2 + x
    d_col = (1 - y) * 2 + (1 - x)
    x_dev = z * 4 + x_col
    y_dev = z * 4 + y_col
    has_up = z < line - 1
    has_down = z > 0
    layer_count, train_rows, _ = ta.shape
    rows = buf.shape[3]
    q_block = Q // layers

    for which, (src, dst) in enumerate(((train_a, ta), (train_g, tg))):
        pltpu.make_async_copy(src, dst, train_sem.at[which]).start()
    for which, src in enumerate((test_a, test_g)):
        pltpu.make_async_copy(src, buf.at[which, :, z * 4], own_sem.at[which]).start()

    barrier = pltpu.get_barrier_semaphore()

    def greet(where):
        pl.semaphore_signal(barrier, inc=1, device_id=where, device_id_type=MESH)

    greet({"tok": x_dev})
    greet({"tok": y_dev})
    pl.when(has_up)(lambda: greet({"tok": me + 4}))
    pl.when(has_down)(lambda: greet({"tok": me - 4}))
    for step in range(1, layers):
        greet({"layer": lax.rem(core + step, layers)})
    ends = jnp.where(has_up, 1, 0) + jnp.where(has_down, 1, 0)
    pl.semaphore_wait(barrier, layers + 1 + ends)

    def copy(route, which, zz, held, there, to, src=None):
        return pltpu.make_async_remote_copy(
            src_ref=buf.at[which, :, zz * 4 + held] if src is None else src,
            dst_ref=buf.at[which, :, zz * 4 + there],
            send_sem=send_sem.at[route, which, zz],
            recv_sem=recv_sem.at[which, zz * 4 + there],
            device_id={"tok": to},
            device_id_type=MESH,
        )

    def arrived(which, zz, there):
        copy(0, which, zz, 0, there, x_dev).wait_recv()

    def nth(i):
        low = z < line - 1 - z
        near = jnp.where(low, z, line - 1 - z)
        half = (i + 1) // 2
        side = jnp.where(i % 2 == 1, z - half, z + half)
        rest = jnp.where(low, i, line - 1 - i)
        return jnp.where(i <= 2 * near, side, rest)

    for which, src in enumerate((test_a, test_g)):
        pl.when(has_up)(lambda: copy(3, which, z, 0, 0, me + 4, src).start())
        pl.when(has_down)(lambda: copy(4, which, z, 0, 0, me - 4, src).start())
        copy(0, which, z, 0, 2, x_dev, src).start()
        copy(1, which, z, 0, 3, y_dev, src).start()

    acc[...] = jnp.zeros_like(acc)
    tile = math.gcd(train_rows, 1024)
    labels = lax.broadcasted_iota(jnp.int32, (Q, rows), 0)
    nt = (((1,), (1,)), ((), ()))

    def accumulate(zz, first, columns):
        one_hot = [
            jnp.where(ids_ref[zz * 4 + c] == labels, 1.0, 0.0).astype(jnp.bfloat16)
            for c in columns
        ]
        select = jnp.concatenate(one_hot * layer_count, axis=1)
        pair = pl.ds(zz * 4 + first, 2)

        def held(which, layer):
            return buf[which, layer, pair].reshape(2 * rows, buf.shape[4])

        def one_tile(j, carry):
            at = pl.ds(pl.multiple_of(j * tile, tile), tile)
            products = []
            for layer in range(layer_count):
                a_gram = lax.dot_general(
                    held(0, layer), ta[layer, at, :], nt, preferred_element_type=jnp.float32
                )
                g_gram = lax.dot_general(
                    held(1, layer), tg[layer, at, :], nt, preferred_element_type=jnp.float32
                )
                products.append((a_gram * g_gram).astype(jnp.bfloat16))
            acc[:, at] += jnp.dot(
                select, jnp.concatenate(products, axis=0), preferred_element_type=jnp.float32
            )
            return carry

        lax.fori_loop(0, train_rows // tile, one_tile, 0)

    for which, (src, dst) in enumerate(((train_a, ta), (train_g, tg))):
        pltpu.make_async_copy(src, dst, train_sem.at[which]).wait()
    for which, src in enumerate((test_a, test_g)):
        pltpu.make_async_copy(src, buf.at[which, :, z * 4], own_sem.at[which]).wait()

    def stage(i, carry):
        zi = nth(i)

        @pl.when(i + 1 < line)
        def _():
            zn = nth(i + 1)
            for which in range(2):
                arrived(which, zn, 0)
                pl.when((zn < z) & has_up)(lambda: copy(3, which, zn, 0, 0, me + 4).start())
                pl.when((zn > z) & has_down)(lambda: copy(4, which, zn, 0, 0, me - 4).start())
                copy(0, which, zn, 0, 2, x_dev).start()
                copy(1, which, zn, 0, 3, y_dev).start()

        @pl.when(i < line)
        def _():
            arrived(0, zi, 2)
            copy(2, 0, zi, 2, 1, y_dev).start()
            arrived(0, zi, 3)
            arrived(1, zi, 3)
            copy(2, 1, zi, 3, 1, x_dev).start()
            arrived(1, zi, 2)
            accumulate(zi, 2, (x_col, y_col))

        @pl.when(i > 0)
        def _():
            zd = nth(i - 1)
            for which in range(2):
                arrived(which, zd, 1)
            accumulate(zd, 0, (own_col, d_col))

        return carry

    lax.fori_loop(0, line + 1, stage, 0)

    def exchange(step):
        to = lax.rem(core + step, layers)
        return pltpu.make_async_remote_copy(
            src_ref=acc.at[pl.ds(pl.multiple_of(to * q_block, q_block), q_block)],
            dst_ref=xbuf.at[step - 1],
            send_sem=xs_sem.at[step - 1],
            recv_sem=xr_sem.at[step - 1],
            device_id={"layer": to},
            device_id_type=MESH,
        )

    for step in range(1, layers):
        exchange(step).start()

    def drain(zz, carry):
        for which in range(2):
            copy(0, which, zz, 0, 2, x_dev).wait_send()
            copy(1, which, zz, 0, 3, y_dev).wait_send()
            copy(2, which, zz, 2, 1, y_dev).wait_send()
            pl.when((zz <= z) & has_up)(lambda: copy(3, which, zz, 0, 0, me + 4).wait_send())
            pl.when((zz >= z) & has_down)(lambda: copy(4, which, zz, 0, 0, me - 4).wait_send())
        return carry

    lax.fori_loop(0, line, drain, 0)

    mine = pl.ds(pl.multiple_of(core * q_block, q_block), q_block)
    for step in range(1, layers):
        exchange(step).wait_recv()
    result = acc[mine, :]
    for step in range(1, layers):
        result = result + xbuf[step - 1]
    out_ref[...] = result
    for step in range(1, layers):
        exchange(step).wait_send()


def on_device(layers, toks, train_act, train_grad, test_act, test_grad, segment_ids):
    layer_count, train_rows, width = train_act.shape
    rows = test_act.shape[1]
    line = toks // 4
    q_block = Q // layers
    ids = segment_ids.reshape(toks, 1, rows)
    dma = pltpu.SemaphoreType.DMA
    anywhere = pl.BlockSpec(memory_space=pl.ANY)
    return pl.pallas_call(
        functools.partial(kernel, layers, line),
        out_shape=jax.ShapeDtypeStruct((q_block, train_rows), jnp.float32),
        in_specs=[anywhere] * 4 + [pl.BlockSpec(memory_space=pltpu.VMEM)],
        out_specs=pl.BlockSpec(memory_space=pltpu.VMEM),
        scratch_shapes=[
            pltpu.VMEM((layer_count, train_rows, width), jnp.bfloat16),
            pltpu.VMEM((layer_count, train_rows, width), jnp.bfloat16),
            pltpu.VMEM((2, layer_count, toks, rows, width), jnp.bfloat16),
            pltpu.VMEM((Q, train_rows), jnp.float32),
            pltpu.VMEM((layers - 1, q_block, train_rows), jnp.float32),
            dma((2,)),
            dma((2,)),
            dma((2, toks)),
            dma((5, 2, line)),
            dma((layers - 1,)),
            dma((layers - 1,)),
        ],
        compiler_params=pltpu.CompilerParams(
            collective_id=0, has_side_effects=True, vmem_limit_bytes=63 * 1024 * 1024
        ),
    )(train_act, train_grad, test_act, test_grad, ids)


def solution(mesh):
    placed = (
        P("layer", "tok", None),
        P("layer", "tok", None),
        P("layer", "tok", None),
        P("layer", "tok", None),
        P(),
    )
    body = functools.partial(on_device, mesh.shape["layer"], mesh.shape["tok"])
    return jax.shard_map(
        body, mesh=mesh, in_specs=placed, out_specs=P("layer", "tok"), check_vma=False
    )
```

```python
import functools
import math

import jax
import jax.numpy as jnp
from jax import lax
from jax.experimental import pallas as pl
from jax.experimental.pallas import tpu as pltpu
from jax.sharding import PartitionSpec as P

Q = 128
MESH = pl.DeviceIdType.MESH


def kernel(
    layers,
    line,
    train_a,
    train_g,
    test_a,
    test_g,
    ids_ref,
    out_ref,
    ta,
    tg,
    buf,
    acc,
    xbuf,
    train_sem,
    own_sem,
    recv_sem,
    send_sem,
    xs_sem,
    xr_sem,
):
    me = lax.axis_index("tok")
    core = lax.axis_index("layer")
    z = me // 4
    y = (me // 2) % 2
    x = me % 2
    own_col = y * 2 + x
    x_col = y * 2 + (1 - x)
    y_col = (1 - y) * 2 + x
    d_col = (1 - y) * 2 + (1 - x)
    x_dev = z * 4 + x_col
    y_dev = z * 4 + y_col
    has_up = z < line - 1
    has_down = z > 0
    layer_count, train_rows, _ = ta.shape
    rows = buf.shape[3]
    q_block = Q // layers

    for which, (src, dst) in enumerate(((train_a, ta), (train_g, tg))):
        pltpu.make_async_copy(src, dst, train_sem.at[which]).start()
    for which, src in enumerate((test_a, test_g)):
        pltpu.make_async_copy(src, buf.at[which, :, z * 4], own_sem.at[which]).start()

    barrier = pltpu.get_barrier_semaphore()

    def greet(where):
        pl.semaphore_signal(barrier, inc=1, device_id=where, device_id_type=MESH)

    greet({"tok": x_dev})
    greet({"tok": y_dev})
    pl.when(has_up)(lambda: greet({"tok": me + 4}))
    pl.when(has_down)(lambda: greet({"tok": me - 4}))
    for step in range(1, layers):
        greet({"layer": lax.rem(core + step, layers)})
    ends = jnp.where(has_up, 1, 0) + jnp.where(has_down, 1, 0)
    pl.semaphore_wait(barrier, layers + 1 + ends)

    def copy(route, which, zz, held, there, to, src=None):
        return pltpu.make_async_remote_copy(
            src_ref=buf.at[which, :, zz * 4 + held] if src is None else src,
            dst_ref=buf.at[which, :, zz * 4 + there],
            send_sem=send_sem.at[route, which, zz],
            recv_sem=recv_sem.at[which, zz * 4 + there],
            device_id={"tok": to},
            device_id_type=MESH,
        )

    def arrived(which, zz, there):
        copy(0, which, zz, 0, there, x_dev).wait_recv()

    def nth(i):
        low = z < line - 1 - z
        near = jnp.where(low, z, line - 1 - z)
        half = (i + 1) // 2
        side = jnp.where(i % 2 == 1, z - half, z + half)
        rest = jnp.where(low, i, line - 1 - i)
        return jnp.where(i <= 2 * near, side, rest)

    for which, src in enumerate((test_a, test_g)):
        pl.when(has_up)(lambda: copy(3, which, z, 0, 0, me + 4, src).start())
        pl.when(has_down)(lambda: copy(4, which, z, 0, 0, me - 4, src).start())
        copy(0, which, z, 0, 2, x_dev, src).start()
        copy(1, which, z, 0, 3, y_dev, src).start()

    acc[...] = jnp.zeros_like(acc)
    _, tiles, _, tile = xbuf.shape
    labels = lax.broadcasted_iota(jnp.int32, (Q, rows), 0)
    nt = (((1,), (1,)), ((), ()))

    def exchange(step, j):
        to = lax.rem(core + step, layers)
        theirs = pl.ds(pl.multiple_of(to * q_block, q_block), q_block)
        return pltpu.make_async_remote_copy(
            src_ref=acc.at[theirs, pl.ds(pl.multiple_of(j * tile, tile), tile)],
            dst_ref=xbuf.at[step - 1, j],
            send_sem=xs_sem.at[step - 1, j],
            recv_sem=xr_sem.at[step - 1, j],
            device_id={"layer": to},
            device_id_type=MESH,
        )

    def accumulate(zz, first, columns, final=None):
        one_hot = [
            jnp.where(ids_ref[zz * 4 + c] == labels, 1.0, 0.0).astype(jnp.bfloat16)
            for c in columns
        ]
        select = jnp.concatenate(one_hot * layer_count, axis=1)
        pair = pl.ds(zz * 4 + first, 2)

        def held(which, layer):
            return buf[which, layer, pair].reshape(2 * rows, buf.shape[4])

        def one_tile(j, carry):
            at = pl.ds(pl.multiple_of(j * tile, tile), tile)
            products = []
            for layer in range(layer_count):
                a_gram = lax.dot_general(
                    held(0, layer), ta[layer, at, :], nt, preferred_element_type=jnp.float32
                )
                g_gram = lax.dot_general(
                    held(1, layer), tg[layer, at, :], nt, preferred_element_type=jnp.float32
                )
                products.append((a_gram * g_gram).astype(jnp.bfloat16))
            acc[:, at] += jnp.dot(
                select, jnp.concatenate(products, axis=0), preferred_element_type=jnp.float32
            )
            if final is not None:

                @pl.when(final)
                def _():
                    for step in range(1, layers):
                        exchange(step, j).start()

            return carry

        lax.fori_loop(0, tiles, one_tile, 0)

    for which, (src, dst) in enumerate(((train_a, ta), (train_g, tg))):
        pltpu.make_async_copy(src, dst, train_sem.at[which]).wait()
    for which, src in enumerate((test_a, test_g)):
        pltpu.make_async_copy(src, buf.at[which, :, z * 4], own_sem.at[which]).wait()

    def stage(i, carry):
        zi = nth(i)

        @pl.when(i + 1 < line)
        def _():
            zn = nth(i + 1)
            for which in range(2):
                arrived(which, zn, 0)
                pl.when((zn < z) & has_up)(lambda: copy(3, which, zn, 0, 0, me + 4).start())
                pl.when((zn > z) & has_down)(lambda: copy(4, which, zn, 0, 0, me - 4).start())
                copy(0, which, zn, 0, 2, x_dev).start()
                copy(1, which, zn, 0, 3, y_dev).start()

        @pl.when(i < line)
        def _():
            arrived(0, zi, 2)
            copy(2, 0, zi, 2, 1, y_dev).start()
            arrived(0, zi, 3)
            arrived(1, zi, 3)
            copy(2, 1, zi, 3, 1, x_dev).start()
            arrived(1, zi, 2)
            accumulate(zi, 2, (x_col, y_col))

        @pl.when(i > 0)
        def _():
            zd = nth(i - 1)
            for which in range(2):
                arrived(which, zd, 1)
            accumulate(zd, 0, (own_col, d_col), i == line)

        return carry

    lax.fori_loop(0, line + 1, stage, 0)

    def drain(zz, carry):
        for which in range(2):
            copy(0, which, zz, 0, 2, x_dev).wait_send()
            copy(1, which, zz, 0, 3, y_dev).wait_send()
            copy(2, which, zz, 2, 1, y_dev).wait_send()
            pl.when((zz <= z) & has_up)(lambda: copy(3, which, zz, 0, 0, me + 4).wait_send())
            pl.when((zz >= z) & has_down)(lambda: copy(4, which, zz, 0, 0, me - 4).wait_send())
        return carry

    lax.fori_loop(0, line, drain, 0)

    mine = pl.ds(pl.multiple_of(core * q_block, q_block), q_block)
    for j in range(tiles):
        at = pl.ds(j * tile, tile)
        for step in range(1, layers):
            exchange(step, j).wait_recv()
        result = acc[mine, at]
        for step in range(1, layers):
            result = result + xbuf[step - 1, j]
        out_ref[:, at] = result
    for j in range(tiles):
        for step in range(1, layers):
            exchange(step, j).wait_send()


def on_device(layers, toks, train_act, train_grad, test_act, test_grad, segment_ids):
    layer_count, train_rows, width = train_act.shape
    rows = test_act.shape[1]
    line = toks // 4
    tile = math.gcd(train_rows, 1024)
    tiles = train_rows // tile
    q_block = Q // layers
    ids = segment_ids.reshape(toks, 1, rows)
    dma = pltpu.SemaphoreType.DMA
    anywhere = pl.BlockSpec(memory_space=pl.ANY)
    return pl.pallas_call(
        functools.partial(kernel, layers, line),
        out_shape=jax.ShapeDtypeStruct((q_block, train_rows), jnp.float32),
        in_specs=[anywhere] * 4 + [pl.BlockSpec(memory_space=pltpu.VMEM)],
        out_specs=pl.BlockSpec(memory_space=pltpu.VMEM),
        scratch_shapes=[
            pltpu.VMEM((layer_count, train_rows, width), jnp.bfloat16),
            pltpu.VMEM((layer_count, train_rows, width), jnp.bfloat16),
            pltpu.VMEM((2, layer_count, toks, rows, width), jnp.bfloat16),
            pltpu.VMEM((Q, train_rows), jnp.float32),
            pltpu.VMEM((layers - 1, tiles, q_block, tile), jnp.float32),
            dma((2,)),
            dma((2,)),
            dma((2, toks)),
            dma((5, 2, line)),
            dma((layers - 1, tiles)),
            dma((layers - 1, tiles)),
        ],
        compiler_params=pltpu.CompilerParams(
            collective_id=0, has_side_effects=True, vmem_limit_bytes=63 * 1024 * 1024
        ),
    )(train_act, train_grad, test_act, test_grad, ids)


def solution(mesh):
    placed = (
        P("layer", "tok", None),
        P("layer", "tok", None),
        P("layer", "tok", None),
        P("layer", "tok", None),
        P(),
    )
    body = functools.partial(on_device, mesh.shape["layer"], mesh.shape["tok"])
    return jax.shard_map(
        body, mesh=mesh, in_specs=placed, out_specs=P("layer", "tok"), check_vma=False
    )
```
